512 devices in a mesh: sweep: 8 (over z_lo), tile: 64 (over z_hi, y, x, core).
Axes of the slice: x: 4, y: 4, z: 16 (z_hi: 2, z_lo: 8; z = z_hi * 8 + z_lo), core: 2. Of those that a mesh axis runs over, the one named last changes fastest.
Arguments:
- adjoint_source: bfloat16 [2, 8, 256, 128, 256], P(None, 'sweep', 'tile'), may hold values from -6 to 6
- forward_field: bfloat16 [2, 8, 256, 128, 256], P(None, 'sweep', 'tile'), may hold values from -6 to 6
- factor_blocks: bfloat16 [8, 256, 3, 2, 128, 128], P('sweep', 'tile')
- factor_index: int32 [8, 256, 3], P('sweep', 'tile'), may hold values from 0 to 7, as said below
- pml_thickness: int32 [256], replicated, may hold values from 1 to 4
Outputs:
- adjoint_field: bfloat16 [2, 8, 256, 128, 256], P(None, 'sweep', 'tile')
- gradient: float32 [8, 256, 128], P('sweep', 'tile')
The draws below stay inside these ranges and needn't reach their ends.
Inputs may be any that keep to these rules, and one draw needn't show every extreme that they name: `factor_index`: each row's 3 numbers differ; the first is 2 + (x mod 4), the row itself, and the second lies among the 2 rows beyond the device's rows on either side.
All inputs are finite; a program needn't handle non-finite values.
Results may differ from the reference program's by a relative error of at most 0.015.
Values may be sent and summed in bfloat16 or wider, within the bound.
A program may use at most 64 MiB of HBM per device.

```python
import math
import jax
import jax.numpy as jnp
from jax import lax

TILE_ROWS = 4
RHS = 256
BLOCK = 128
NONZERO = 3
REACH = 2
GRID_Z = 8
GRID_X = 256


def draw_factor_index(key, part):
    extent = TILE_ROWS + 2 * REACH
    topmost = (1 << 20) * extent
    base = jax.random.randint(key, (GRID_Z, GRID_X, extent), 0, 1 << 20) * extent + jnp.arange(extent, dtype=jnp.int32)[None, None, :]
    position = jnp.arange(GRID_X, dtype=jnp.int32) % TILE_ROWS
    own_row = REACH + position
    picks = jax.random.randint(jax.random.fold_in(key, 7), (GRID_Z, GRID_X), 0, 2 * REACH)
    forced = jnp.where(picks < REACH, picks, picks + TILE_ROWS)
    forced = jnp.where(position[None, :] == 0, 0, jnp.where(position[None, :] == TILE_ROWS - 1, extent - 1, forced))
    column_ids = jnp.arange(extent, dtype=jnp.int32)[None, None, :]
    scores = jnp.where(column_ids == own_row[None, :, None], topmost + 2, base)
    scores = jnp.where(column_ids == forced[:, :, None], topmost + 1, scores)
    _, chosen = lax.top_k(scores, NONZERO)
    return chosen.astype(jnp.int32)


def draw_factor_blocks(key, part):
    shape = (GRID_Z, GRID_X, NONZERO, 2, BLOCK, BLOCK)
    spread = 0.6 / math.sqrt(BLOCK)
    noise = jax.random.normal(key, shape, jnp.float32) * spread
    identity = (jnp.arange(BLOCK)[:, None] == jnp.arange(BLOCK)[None, :]).astype(jnp.float32)
    leading = ((jnp.arange(NONZERO) == 0)[:, None] & (jnp.arange(2) == 0)[None, :]).astype(jnp.float32)
    return (noise + leading[:, :, None, None] * identity).astype(jnp.bfloat16)


def plant(drawn, own_key, least, high):
    dims = drawn.shape
    index_at = [jax.random.randint(jax.random.fold_in(own_key, axis), (), 0, dims[axis]) for axis in range(len(dims))]
    drawn = drawn.at[tuple(index_at)].set(least)
    longest = dims.index(max(dims))
    index_at[longest] = (index_at[longest] + 1) % dims[longest]
    return drawn.at[tuple(index_at)].set(high)


def levels(stream_key, dims, cuts, least, top_value):
    factor_of, own = 1.0, jax.random.fold_in(stream_key, 6)
    for axis_at, blocks in cuts:
        steps = jnp.exp(jax.random.uniform(jax.random.fold_in(own, axis_at), (blocks,), jnp.float32, least / len(cuts), top_value / len(cuts)))
        factor_of = factor_of * jnp.repeat(steps, dims[axis_at] // blocks).reshape([-1 if axis == axis_at else 1 for axis in range(len(dims))])
    return factor_of


def bell_draw(stream_key, shape, deviation, bound, pieces=(), kind=jnp.bfloat16):
    array = deviation * jax.random.normal(stream_key, shape, jnp.float32)
    if pieces:
        array = array * levels(stream_key, shape, pieces, -0.22, 0.18)
    return jnp.clip(array, -bound, bound).astype(kind)


def setup_inputs(seed: int = 0) -> dict:
    splits = jax.random.split(jax.random.key(seed), 6)
    return {
        "adjoint_source": bell_draw(splits[0], (2, GRID_Z, GRID_X, BLOCK, RHS), 1.0, 6.0, ((1, 8), (2, 64))),
        "forward_field": bell_draw(splits[1], (2, GRID_Z, GRID_X, BLOCK, RHS), 1.0, 6.0, ((1, 8), (2, 64))),
        "factor_blocks": draw_factor_blocks(jax.random.fold_in(splits[5], 71), 0),
        "factor_index": draw_factor_index(jax.random.fold_in(splits[5], 71), 0),
        "pml_thickness": plant(jax.random.randint(splits[4], (RHS,), 1, GRID_Z // 2 + 1), jax.random.fold_in(splits[4], 1), 1, (GRID_Z // 2 + 1) - 1).astype(jnp.int32),
    }


lateral_weight = 0.25
pml_factor = 0.55

def laplace(extended):
    center = extended[:, 1:-1]
    padded = jnp.pad(center, ((0, 0), (0, 0), (1, 1), (0, 0)))
    return extended[:, 2:] + extended[:, :-2] + padded[:, :, 2:] + padded[:, :, :-2] - 4.0 * center

def reference(adjoint_source, forward_field, factor_blocks, factor_index, pml_thickness):
    thickness = pml_thickness
    depth_z = adjoint_source.shape[1]
    grid_x = adjoint_source.shape[2]
    norm_scale = 1.0 / math.sqrt(adjoint_source.shape[4])
    tile_start = (jnp.arange(grid_x, dtype=jnp.int32) // TILE_ROWS * TILE_ROWS).astype(jnp.int32)
    sources = jnp.moveaxis(adjoint_source, 1, 0)
    forwards = jnp.moveaxis(forward_field, 1, 0)

    def layer_step(previous, inputs):
        source_layer, forward_layer, blocks, indices, depth_pos = inputs
        extended = jnp.pad(previous.astype(jnp.float32), ((0, 0), (1, 1), (0, 0), (0, 0)))
        in_pml = (depth_pos < thickness) | (depth_pos >= depth_z - thickness)
        layer_gain = jnp.where(in_pml, pml_factor, 1.0).astype(jnp.float32)
        own_w = (source_layer.astype(jnp.float32) - layer_gain * (extended[:, 1:-1] + lateral_weight * laplace(extended))).astype(jnp.bfloat16)
        padded_w = jnp.pad(own_w, ((0, 0), (REACH, REACH), (0, 0), (0, 0)))
        columns = (tile_start[:, None] + indices).astype(jnp.int32)
        picked = jnp.take(padded_w, columns, axis=1)
        terms = jnp.einsum('xkcij,dxkjr->cdxir', blocks.astype(jnp.float32), picked.astype(jnp.float32))
        real_part = terms[0, 0] - terms[1, 1]
        imag_part = terms[0, 1] + terms[1, 0]
        current = jnp.stack([real_part, imag_part]).astype(jnp.bfloat16)
        contribution = lax.optimization_barrier(jnp.sum(forward_layer.astype(jnp.float32) * current.astype(jnp.float32), axis=(0, 3))) * norm_scale
        return (current, (current, contribution))
    initial = jnp.zeros(sources.shape[1:], jnp.bfloat16)
    depths = jnp.arange(depth_z, dtype=jnp.int32)
    _, (adjoint, gradient) = lax.scan(layer_step, initial, (sources, forwards, factor_blocks, factor_index, depths), reverse=True)
    return (jnp.moveaxis(adjoint, 0, 1), gradient)
```

```python
import functools
import math

import jax
import jax.numpy as jnp
from jax import lax
from jax.experimental import pallas as pl
from jax.experimental.pallas import tpu as pltpu
from jax.sharding import PartitionSpec as P

PML_FACTOR = 0.55
LATERAL_WEIGHT = 0.25
CHUNK = 32
DEPTH = 1
NT = (((1,), (1,)), ((), ()))


def sweep_kernel(
    sweeps,
    tiles,
    idx_ref,
    thick_ref,
    src_hbm,
    fwd_hbm,
    fac_hbm,
    out_hbm,
    grad_ref,
    s_nat,
    f_nat,
    fac,
    s_t,
    gq,
    mats,
    vin,
    vout,
    onat,
    part,
    wext,
    hsend,
    hrecv,
    load_sem,
    zsend_sem,
    zrecv_sem,
    hsend_sem,
    hrecv_sem,
    out_sem,
):
    rows, rhs, wide = vin.shape
    block = wide // 2
    nonzero = mats.shape[1]
    chunks = rhs // CHUNK
    z = lax.axis_index("sweep")
    t = lax.axis_index("tile")
    has_left = t > 0
    has_right = t < tiles - 1
    has_above = z < sweeps - 1
    has_below = z > 0
    left = jnp.maximum(t - 1, 0)
    right = jnp.minimum(t + 1, tiles - 1)
    below = jnp.maximum(z - 1, 0)

    loads = [
        pltpu.make_async_copy(src_hbm, s_nat, load_sem.at[0]),
        pltpu.make_async_copy(fac_hbm, fac, load_sem.at[1]),
        pltpu.make_async_copy(fwd_hbm, f_nat, load_sem.at[2]),
    ]
    for copy in loads:
        copy.start()

    barrier = pltpu.get_barrier_semaphore()

    @pl.when(has_above)
    def _():
        pl.semaphore_signal(barrier, inc=1, device_id={"sweep": jnp.minimum(z + 1, sweeps - 1)})

    @pl.when(has_left)
    def _():
        pl.semaphore_signal(barrier, inc=1, device_id={"tile": left})

    @pl.when(has_right)
    def _():
        pl.semaphore_signal(barrier, inc=1, device_id={"tile": right})

    thick = thick_ref[...]
    in_pml = (z < thick) | (z >= sweeps - thick)
    gain = jnp.where(in_pml, PML_FACTOR * LATERAL_WEIGHT, LATERAL_WEIGHT).astype(jnp.float32)
    gq[...] = jnp.transpose(jnp.broadcast_to(gain, (block, rhs)), (1, 0))

    @pl.when(jnp.logical_not(has_above))
    def _():
        vin[...] = jnp.zeros_like(vin)

    @pl.when(jnp.logical_not(has_left))
    def _():
        hrecv[0] = jnp.zeros(hrecv.shape[1:], hrecv.dtype)

    @pl.when(jnp.logical_not(has_right))
    def _():
        hrecv[1] = jnp.zeros(hrecv.shape[1:], hrecv.dtype)

    loads[0].wait()

    def turn_source(x, carry):
        for c in range(2):
            s_t[x, :, c * block : (c + 1) * block] = jnp.transpose(s_nat[c, 0, x], (1, 0))
        return carry

    lax.fori_loop(0, rows, turn_source, 0)

    loads[1].wait()

    def build(x, carry):
        for k in range(nonzero):
            re = fac[0, x, k, 0]
            im = fac[0, x, k, 1]
            mats[x, k, :block, :block] = re
            mats[x, k, :block, block:] = -im
            mats[x, k, block:, :block] = im
            mats[x, k, block:, block:] = re
        return carry

    lax.fori_loop(0, rows, build, 0)

    pl.semaphore_wait(
        barrier,
        has_below.astype(jnp.int32) + has_left.astype(jnp.int32) + has_right.astype(jnp.int32),
    )

    lane = lax.broadcasted_iota(jnp.int32, (CHUNK, block), 1)
    left_on = has_left.astype(jnp.float32)
    right_on = has_right.astype(jnp.float32)

    def span(g):
        return pl.ds(pl.multiple_of(g * CHUNK, CHUNK), CHUNK)

    def hand_down(g):
        return pltpu.make_async_remote_copy(
            src_ref=vout.at[:, span(g)],
            dst_ref=vin.at[:, span(g)],
            send_sem=zsend_sem.at[g],
            recv_sem=zrecv_sem.at[g],
            device_id={"sweep": below},
        )

    def to_left(g):
        return pltpu.make_async_remote_copy(
            src_ref=hsend.at[0, :, span(g)],
            dst_ref=hrecv.at[1, :, span(g)],
            send_sem=hsend_sem.at[0, g],
            recv_sem=hrecv_sem.at[1, g],
            device_id={"tile": left},
        )

    def to_right(g):
        return pltpu.make_async_remote_copy(
            src_ref=hsend.at[1, :, span(g)],
            dst_ref=hrecv.at[0, :, span(g)],
            send_sem=hsend_sem.at[1, g],
            recv_sem=hrecv_sem.at[0, g],
            device_id={"tile": right},
        )

    def edges_out(g):
        rs = span(g)

        @pl.when(has_above)
        def _():
            hand_down(g).wait_recv()

        scale = gq[rs, :]
        for c in range(2):
            ls = slice(c * block, (c + 1) * block)
            v = [vin[x, rs, ls].astype(jnp.float32) for x in range(rows)]
            for x in range(rows):
                up = jnp.where(lane == block - 1, 0.0, pltpu.roll(v[x], block - 1, 1))
                down = jnp.where(lane == 0, 0.0, pltpu.roll(v[x], 1, 1))
                total = up + down
                if x > 0:
                    total = total + v[x - 1]
                if x < rows - 1:
                    total = total + v[x + 1]
                w = s_t[x, rs, ls].astype(jnp.float32) - scale * total
                low = w.astype(jnp.bfloat16)
                if x == 0:
                    part[0, rs, ls] = w
                    hsend[0, 1, rs, ls] = low
                    hsend[0, 0, rs, ls] = vin[0, rs, ls]
                elif x == rows - 1:
                    part[1, rs, ls] = w
                    hsend[1, 1, rs, ls] = low
                    hsend[1, 0, rs, ls] = vin[rows - 1, rs, ls]
                else:
                    wext[2 + x, rs, ls] = low
                    if x == 1:
                        hsend[0, 2, rs, ls] = low
                    if x == rows - 2:
                        hsend[1, 2, rs, ls] = low

        @pl.when(has_left)
        def _():
            to_left(g).start()

        @pl.when(has_right)
        def _():
            to_right(g).start()

    def rows_out(g):
        rs = span(g)

        @pl.when(has_left)
        def _():
            to_right(g).wait_recv()

        @pl.when(has_right)
        def _():
            to_left(g).wait_recv()

        scale = gq[rs, :]
        for c in range(2):
            ls = slice(c * block, (c + 1) * block)
            near = hrecv[0, 0, rs, ls].astype(jnp.float32)
            wext[2, rs, ls] = (part[0, rs, ls] - scale * near).astype(jnp.bfloat16)
            near = hrecv[1, 0, rs, ls].astype(jnp.float32)
            wext[rows + 1, rs, ls] = (part[1, rs, ls] - scale * near).astype(jnp.bfloat16)
            mine = vin[0, rs, ls].astype(jnp.float32) * left_on
            wext[1, rs, ls] = (hrecv[0, 1, rs, ls].astype(jnp.float32) - scale * mine).astype(
                jnp.bfloat16
            )
            mine = vin[rows - 1, rs, ls].astype(jnp.float32) * right_on
            wext[rows + 2, rs, ls] = (
                hrecv[1, 1, rs, ls].astype(jnp.float32) - scale * mine
            ).astype(jnp.bfloat16)
            wext[0, rs, ls] = hrecv[0, 2, rs, ls]
            wext[rows + 3, rs, ls] = hrecv[1, 2, rs, ls]
        for x in range(rows):
            acc = None
            for k in range(nonzero):
                term = lax.dot_general(
                    wext[idx_ref[x, k], rs, :],
                    mats[x, k],
                    NT,
                    preferred_element_type=jnp.float32,
                )
                acc = term if acc is None else acc + term
            vout[x, rs, :] = acc.astype(jnp.bfloat16)

        @pl.when(has_below)
        def _():
            hand_down(g).start()

    for g in range(DEPTH):
        edges_out(jnp.int32(g))

    def step(g, carry):
        @pl.when(g + DEPTH < chunks)
        def _():
            edges_out(g + DEPTH)

        rows_out(g)
        return carry

    lax.fori_loop(0, chunks, step, 0)

    loads[2].wait()

    norm_scale = 1.0 / math.sqrt(rhs)

    def finish(x, carry):
        total = jnp.zeros((block, block), jnp.float32)
        for c in range(2):
            for h in range(rhs // block):
                hs = slice(h * block, (h + 1) * block)
                turned = jnp.transpose(vout[x, hs, c * block : (c + 1) * block], (1, 0))
                onat[c, 0, x, :, hs] = turned
                total = total + f_nat[c, 0, x, :, hs].astype(jnp.float32) * turned.astype(
                    jnp.float32
                )
        turned = jnp.transpose(total, (1, 0))
        grad_ref[x] = jnp.sum(turned, axis=0, keepdims=True) * norm_scale
        return carry

    lax.fori_loop(0, rows, finish, 0)

    store = pltpu.make_async_copy(onat, out_hbm, out_sem)
    store.start()

    def drain(g, carry):
        @pl.when(has_below)
        def _():
            hand_down(g).wait_send()

        @pl.when(has_left)
        def _():
            to_left(g).wait_send()

        @pl.when(has_right)
        def _():
            to_right(g).wait_send()

        return carry

    lax.fori_loop(0, chunks, drain, 0)
    store.wait()


def on_device(sweeps, tiles, adjoint_source, forward_field, factor_blocks, factor_index, pml_thickness):
    _, layers, rows, block, rhs = adjoint_source.shape
    assert layers == 1
    nonzero = factor_blocks.shape[2]
    wide = 2 * block
    chunks = rhs // CHUNK
    bf16 = jnp.bfloat16
    f32 = jnp.float32
    any_spec = pl.BlockSpec(memory_space=pl.ANY)
    vmem_spec = pl.BlockSpec(memory_space=pltpu.VMEM)
    adjoint, gradient = pl.pallas_call(
        functools.partial(sweep_kernel, sweeps, tiles),
        out_shape=(
            jax.ShapeDtypeStruct(adjoint_source.shape, bf16),
            jax.ShapeDtypeStruct((rows, 1, block), f32),
        ),
        in_specs=[
            pl.BlockSpec(memory_space=pltpu.SMEM),
            vmem_spec,
            any_spec,
            any_spec,
            any_spec,
        ],
        out_specs=(any_spec, vmem_spec),
        scratch_shapes=[
            pltpu.VMEM(adjoint_source.shape, bf16),
            pltpu.VMEM(forward_field.shape, bf16),
            pltpu.VMEM(factor_blocks.shape, bf16),
            pltpu.VMEM((rows, rhs, wide), bf16),
            pltpu.VMEM((rhs, block), f32),
            pltpu.VMEM((rows, nonzero, wide, wide), bf16),
            pltpu.VMEM((rows, rhs, wide), bf16),
            pltpu.VMEM((rows, rhs, wide), bf16),
            pltpu.VMEM(adjoint_source.shape, bf16),
            pltpu.VMEM((2, rhs, wide), f32),
            pltpu.VMEM((rows + 4, rhs, wide), bf16),
            pltpu.VMEM((2, 3, rhs, wide), bf16),
            pltpu.VMEM((2, 3, rhs, wide), bf16),
            pltpu.SemaphoreType.DMA((3,)),
            pltpu.SemaphoreType.DMA((chunks,)),
            pltpu.SemaphoreType.DMA((chunks,)),
            pltpu.SemaphoreType.DMA((2, chunks)),
            pltpu.SemaphoreType.DMA((2, chunks)),
            pltpu.SemaphoreType.DMA,
        ],
        compiler_params=pltpu.CompilerParams(
            collective_id=0, has_side_effects=True, vmem_limit_bytes=40 * 1024 * 1024
        ),
    )(
        factor_index[0],
        pml_thickness[None],
        adjoint_source,
        forward_field,
        factor_blocks,
    )
    return adjoint, gradient.reshape(1, rows, block)


def solution(mesh):
    placed = (
        P(None, "sweep", "tile", None, None),
        P(None, "sweep", "tile", None, None),
        P("sweep", "tile", None, None, None, None),
        P("sweep", "tile", None),
        P(),
    )
    return jax.shard_map(
        functools.partial(on_device, mesh.shape["sweep"], mesh.shape["tile"]),
        mesh=mesh,
        in_specs=placed,
        out_specs=(P(None, "sweep", "tile", None, None), P("sweep", "tile", None)),
        check_vma=False,
    )
```

```python
import functools
import math

import jax
import jax.numpy as jnp
from jax import lax
from jax.experimental import pallas as pl
from jax.experimental.pallas import tpu as pltpu
from jax.sharding import PartitionSpec as P

PML_FACTOR = 0.55
LATERAL_WEIGHT = 0.25
CHUNK = 32
DEPTH = 2
NT = (((1,), (1,)), ((), ()))


def sweep_kernel(
    sweeps,
    tiles,
    idx_hbm,
    thick_hbm,
    src_hbm,
    fwd_hbm,
    fac_hbm,
    out_ref,
    grad_ref,
    idx_ref,
    thick_ref,
    s_nat,
    f_nat,
    fac,
    s_t,
    s_next,
    gq,
    gq_next,
    mats,
    vin,
    vout,
    part,
    wext,
    hsend,
    fsend,
    hrecv,
    load_sem,
    up_sem,
    zsend_sem,
    zrecv_sem,
    hsend_sem,
    hrecv_sem,
    fsend_sem,
):
    rows, rhs, wide = vin.shape
    block = wide // 2
    nonzero = mats.shape[1]
    chunks = rhs // CHUNK
    z = lax.axis_index("sweep")
    t = lax.axis_index("tile")
    has_left = t > 0
    has_right = t < tiles - 1
    has_above = z < sweeps - 1
    has_below = z > 0
    top = jnp.logical_not(has_above)
    far_left = t == tiles // 2
    far_right = t == tiles // 2 - 1
    is_far = far_left | far_right
    send_left = has_left & (jnp.logical_not(far_left) | top)
    send_right = has_right & (jnp.logical_not(far_right) | top)
    left = jnp.maximum(t - 1, 0)
    right = jnp.minimum(t + 1, tiles - 1)
    below = jnp.maximum(z - 1, 0)
    above = jnp.minimum(z + 1, sweeps - 1)
    partner = jnp.where(far_left, left, right)
    partner_side = far_left.astype(jnp.int32)

    loads = [
        pltpu.make_async_copy(src_hbm, s_nat, load_sem.at[0]),
        pltpu.make_async_copy(thick_hbm, thick_ref, load_sem.at[1]),
        pltpu.make_async_copy(idx_hbm, idx_ref, load_sem.at[2]),
        pltpu.make_async_copy(fac_hbm, fac, load_sem.at[3]),
        pltpu.make_async_copy(fwd_hbm, f_nat, load_sem.at[4]),
    ]

    barrier = pltpu.get_barrier_semaphore()

    def greet(wanted, **device_id):
        @pl.when(wanted)
        def _():
            pl.semaphore_signal(barrier, inc=1, device_id=device_id)

    greet(is_far & has_above, sweep=above, tile=partner)
    greet(send_left, tile=left)
    greet(send_right, tile=right)
    greet(has_above, sweep=above)
    greet(is_far & has_below, sweep=below)

    for copy in loads:
        copy.start()

    def gain_rows(depth):
        thick = thick_ref[...]
        in_pml = (depth < thick) | (depth >= sweeps - thick)
        gain = jnp.where(in_pml, PML_FACTOR * LATERAL_WEIGHT, LATERAL_WEIGHT).astype(jnp.float32)
        return jnp.transpose(jnp.broadcast_to(gain, (block, rhs)), (1, 0))

    @pl.when(top)
    def _():
        vin[...] = jnp.zeros_like(vin)

    @pl.when(jnp.logical_not(has_left))
    def _():
        hrecv[0] = jnp.zeros(hrecv.shape[1:], hrecv.dtype)

    @pl.when(jnp.logical_not(has_right))
    def _():
        hrecv[1] = jnp.zeros(hrecv.shape[1:], hrecv.dtype)

    loads[1].wait()
    gq[...] = gain_rows(z)
    loads[0].wait()

    def turn_source(x, carry):
        for c in range(2):
            s_t[x, :, c * block : (c + 1) * block] = jnp.transpose(s_nat[c, 0, x], (1, 0))
        return carry

    lax.fori_loop(0, rows, turn_source, 0)

    def build(x, carry):
        for k in range(nonzero):
            re = fac[0, x, k, 0]
            im = fac[0, x, k, 1]
            mats[x, k, :block, :block] = re
            mats[x, k, :block, block:] = -im
            mats[x, k, block:, :block] = im
            mats[x, k, block:, block:] = re
        return carry

    one = [
        wanted.astype(jnp.int32)
        for wanted in (has_below, send_left, send_right, is_far & has_below, is_far & has_above)
    ]
    pl.semaphore_wait(barrier, one[0] + one[1] + one[2] + one[3] + one[4])

    lane = lax.broadcasted_iota(jnp.int32, (CHUNK, block), 1)
    left_on = has_left.astype(jnp.float32)
    right_on = has_right.astype(jnp.float32)

    def beside(v):
        up = jnp.where(lane == block - 1, 0.0, pltpu.roll(v, block - 1, 1))
        down = jnp.where(lane == 0, 0.0, pltpu.roll(v, 1, 1))
        return up + down

    hand_up = pltpu.make_async_remote_copy(
        src_ref=s_t.at[pl.ds(jnp.where(far_left, 0, rows - 2), 2)],
        dst_ref=s_next,
        send_sem=up_sem.at[0],
        recv_sem=up_sem.at[1],
        device_id={"sweep": above},
    )

    @pl.when(is_far & has_above)
    def _():
        hand_up.start()

    def span(g):
        return pl.ds(pl.multiple_of(g * CHUNK, CHUNK), CHUNK)

    def hand_down(g):
        return pltpu.make_async_remote_copy(
            src_ref=vout.at[:, span(g)],
            dst_ref=vin.at[:, span(g)],
            send_sem=zsend_sem.at[g],
            recv_sem=zrecv_sem.at[g],
            device_id={"sweep": below},
        )

    def to_left(g):
        return pltpu.make_async_remote_copy(
            src_ref=hsend.at[0, :, span(g)],
            dst_ref=hrecv.at[1, :, span(g)],
            send_sem=hsend_sem.at[0, g],
            recv_sem=hrecv_sem.at[1, g],
            device_id={"tile": left},
        )

    def to_right(g):
        return pltpu.make_async_remote_copy(
            src_ref=hsend.at[1, :, span(g)],
            dst_ref=hrecv.at[0, :, span(g)],
            send_sem=hsend_sem.at[1, g],
            recv_sem=hrecv_sem.at[0, g],
            device_id={"tile": right},
        )

    def to_partner(g):
        return pltpu.make_async_remote_copy(
            src_ref=fsend.at[:, span(g)],
            dst_ref=hrecv.at[partner_side, :, span(g)],
            send_sem=fsend_sem.at[g],
            recv_sem=hrecv_sem.at[partner_side, g],
            device_id={"sweep": below, "tile": partner},
        )

    def edges_out(g):
        rs = span(g)

        @pl.when(has_above)
        def _():
            hand_down(g).wait_recv()

        scale = gq[rs, :]
        for c in range(2):
            ls = slice(c * block, (c + 1) * block)
            v = [vin[x, rs, ls].astype(jnp.float32) for x in range(rows)]
            for x in range(rows):
                total = beside(v[x])
                if x > 0:
                    total = total + v[x - 1]
                if x < rows - 1:
                    total = total + v[x + 1]
                w = s_t[x, rs, ls].astype(jnp.float32) - scale * total
                low = w.astype(jnp.bfloat16)
                if x == 0:
                    part[0, rs, ls] = w
                    hsend[0, 1, rs, ls] = low
                    hsend[0, 0, rs, ls] = vin[0, rs, ls]
                elif x == rows - 1:
                    part[1, rs, ls] = w
                    hsend[1, 1, rs, ls] = low
                    hsend[1, 0, rs, ls] = vin[rows - 1, rs, ls]
                else:
                    wext[2 + x, rs, ls] = low
                    if x == 1:
                        hsend[0, 2, rs, ls] = low
                    if x == rows - 2:
                        hsend[1, 2, rs, ls] = low

        @pl.when(send_left)
        def _():
            to_left(g).start()

        @pl.when(send_right)
        def _():
            to_right(g).start()

    def rows_out(g):
        rs = span(g)

        @pl.when(has_left)
        def _():
            to_right(g).wait_recv()

        @pl.when(has_right)
        def _():
            to_left(g).wait_recv()

        scale = gq[rs, :]
        for c in range(2):
            ls = slice(c * block, (c + 1) * block)
            near = hrecv[0, 0, rs, ls].astype(jnp.float32)
            wext[2, rs, ls] = (part[0, rs, ls] - scale * near).astype(jnp.bfloat16)
            near = hrecv[1, 0, rs, ls].astype(jnp.float32)
            wext[rows + 1, rs, ls] = (part[1, rs, ls] - scale * near).astype(jnp.bfloat16)
            mine = vin[0, rs, ls].astype(jnp.float32) * left_on
            wext[1, rs, ls] = (hrecv[0, 1, rs, ls].astype(jnp.float32) - scale * mine).astype(
                jnp.bfloat16
            )
            mine = vin[rows - 1, rs, ls].astype(jnp.float32) * right_on
            wext[rows + 2, rs, ls] = (
                hrecv[1, 1, rs, ls].astype(jnp.float32) - scale * mine
            ).astype(jnp.bfloat16)
            wext[0, rs, ls] = hrecv[0, 2, rs, ls]
            wext[rows + 3, rs, ls] = hrecv[1, 2, rs, ls]
        for j in range(rows):
            x = jnp.where(far_right, rows - 1 - j, j)
            acc = None
            for k in range(nonzero):
                term = lax.dot_general(
                    wext[idx_ref[k, 0, x], rs, :],
                    mats[x, k],
                    NT,
                    preferred_element_type=jnp.float32,
                )
                acc = term if acc is None else acc + term
            vout[x, rs, :] = acc.astype(jnp.bfloat16)
            if j == rows - 2:
                @pl.when(is_far & has_below)
                def _():
                    step_in = jnp.where(far_right, -1, 1)
                    edge = jnp.where(far_right, rows - 1, 0)
                    s_edge = jnp.where(far_right, 1, 0)
                    scale = gq_next[rs, :]
                    for c in range(2):
                        ls = slice(c * block, (c + 1) * block)
                        v0 = vout[edge, rs, ls].astype(jnp.float32)
                        v1 = vout[edge + step_in, rs, ls].astype(jnp.float32)
                        v2 = vout[edge + 2 * step_in, rs, ls].astype(jnp.float32)
                        s0 = s_next[s_edge, rs, ls].astype(jnp.float32)
                        s1 = s_next[1 - s_edge, rs, ls].astype(jnp.float32)
                        fsend[0, rs, ls] = vout[edge, rs, ls]
                        fsend[1, rs, ls] = (s0 - scale * (v1 + beside(v0))).astype(jnp.bfloat16)
                        fsend[2, rs, ls] = (s1 - scale * (v0 + v2 + beside(v1))).astype(
                            jnp.bfloat16
                        )
                    to_partner(g).start()

        @pl.when(has_below)
        def _():
            hand_down(g).start()

    def first_edges(g, carry):
        edges_out(g)
        return carry

    ahead = jnp.where(top, chunks, DEPTH)
    lax.fori_loop(0, jnp.where(top, chunks, 0), first_edges, 0)

    loads[3].wait()
    loads[2].wait()
    lax.fori_loop(0, rows, build, 0)

    @pl.when(is_far & has_below)
    def _():
        gq_next[...] = gain_rows(z - 1)
        hand_up.wait_recv()

    lax.fori_loop(0, jnp.where(top, 0, DEPTH), first_edges, 0)

    def step(g, carry):
        @pl.when(g + ahead < chunks)
        def _():
            edges_out(g + ahead)

        rows_out(g)
        return carry

    lax.fori_loop(0, chunks, step, 0)

    loads[4].wait()

    norm_scale = 1.0 / math.sqrt(rhs)

    def finish(x, carry):
        total = jnp.zeros((block, block), jnp.float32)
        for c in range(2):
            for h in range(rhs // block):
                hs = slice(h * block, (h + 1) * block)
                turned = jnp.transpose(vout[x, hs, c * block : (c + 1) * block], (1, 0))
                out_ref[c, 0, x, :, hs] = turned
                total = total + f_nat[c, 0, x, :, hs].astype(jnp.float32) * turned.astype(
                    jnp.float32
                )
        turned = jnp.transpose(total, (1, 0))
        grad_ref[0, pl.ds(x, 1), :] = jnp.sum(turned, axis=0, keepdims=True) * norm_scale
        return carry

    lax.fori_loop(0, rows, finish, 0)

    @pl.when(is_far & has_above)
    def _():
        hand_up.wait_send()

    def drain(g, carry):
        @pl.when(has_below)
        def _():
            hand_down(g).wait_send()

        @pl.when(is_far & has_below)
        def _():
            to_partner(g).wait_send()

        @pl.when(send_left)
        def _():
            to_left(g).wait_send()

        @pl.when(send_right)
        def _():
            to_right(g).wait_send()

        return carry

    lax.fori_loop(0, chunks, drain, 0)


def on_device(sweeps, tiles, adjoint_source, forward_field, factor_blocks, factor_index, pml_thickness):
    _, layers, rows, block, rhs = adjoint_source.shape
    assert layers == 1
    nonzero = factor_blocks.shape[2]
    wide = 2 * block
    chunks = rhs // CHUNK
    bf16 = jnp.bfloat16
    f32 = jnp.float32
    hbm_spec = pl.BlockSpec(memory_space=pltpu.HBM)
    vmem_spec = pl.BlockSpec(memory_space=pltpu.VMEM)
    index = jnp.transpose(factor_index, (2, 0, 1))
    thickness = pml_thickness[None]
    adjoint, gradient = pl.pallas_call(
        functools.partial(sweep_kernel, sweeps, tiles),
        out_shape=(
            jax.ShapeDtypeStruct(adjoint_source.shape, bf16),
            jax.ShapeDtypeStruct((1, rows, block), f32),
        ),
        in_specs=[hbm_spec] * 5,
        out_specs=(vmem_spec, vmem_spec),
        scratch_shapes=[
            pltpu.SMEM(index.shape, jnp.int32),
            pltpu.VMEM(thickness.shape, jnp.int32),
            pltpu.VMEM(adjoint_source.shape, bf16),
            pltpu.VMEM(forward_field.shape, bf16),
            pltpu.VMEM(factor_blocks.shape, bf16),
            pltpu.VMEM((rows, rhs, wide), bf16),
            pltpu.VMEM((2, rhs, wide), bf16),
            pltpu.VMEM((rhs, block), f32),
            pltpu.VMEM((rhs, block), f32),
            pltpu.VMEM((rows, nonzero, wide, wide), bf16),
            pltpu.VMEM((rows, rhs, wide), bf16),
            pltpu.VMEM((rows, rhs, wide), bf16),
            pltpu.VMEM((2, rhs, wide), f32),
            pltpu.VMEM((rows + 4, rhs, wide), bf16),
            pltpu.VMEM((2, 3, rhs, wide), bf16),
            pltpu.VMEM((3, rhs, wide), bf16),
            pltpu.VMEM((2, 3, rhs, wide), bf16),
            pltpu.SemaphoreType.DMA((5,)),
            pltpu.SemaphoreType.DMA((2,)),
            pltpu.SemaphoreType.DMA((chunks,)),
            pltpu.SemaphoreType.DMA((chunks,)),
            pltpu.SemaphoreType.DMA((2, chunks)),
            pltpu.SemaphoreType.DMA((2, chunks)),
            pltpu.SemaphoreType.DMA((chunks,)),
        ],
        compiler_params=pltpu.CompilerParams(
            collective_id=0, has_side_effects=True, vmem_limit_bytes=63 * 1024 * 1024
        ),
    )(index, thickness, adjoint_source, forward_field, factor_blocks)
    return adjoint, gradient


def solution(mesh):
    placed = (
        P(None, "sweep", "tile", None, None),
        P(None, "sweep", "tile", None, None),
        P("sweep", "tile", None, None, None, None),
        P("sweep", "tile", None),
        P(),
    )
    return jax.shard_map(
        functools.partial(on_device, mesh.shape["sweep"], mesh.shape["tile"]),
        mesh=mesh,
        in_specs=placed,
        out_specs=(P(None, "sweep", "tile", None, None), P("sweep", "tile", None)),
        check_vma=False,
    )
```

```python
import functools
import math

import jax
import jax.numpy as jnp
from jax import lax
from jax.experimental import pallas as pl
from jax.experimental.pallas import tpu as pltpu
from jax.sharding import PartitionSpec as P

PML_FACTOR = 0.55
LATERAL_WEIGHT = 0.25
CHUNK = 32
DEPTH = 2
FAR_EVERY = 8


def sweep_kernel(
    sweeps,
    tiles,
    idx_hbm,
    thick_hbm,
    src_hbm,
    fac_hbm,
    fwd_hbm,
    out_hbm,
    grad_hbm,
    idx_ref,
    thick_ref,
    s_nat,
    f_nat,
    o_nat,
    grad,
    fac,
    s_t,
    s_next,
    gq,
    gq_next,
    mats,
    vin,
    vout,
    part,
    wext,
    hsend,
    fsend,
    hrecv,
    load_sem,
    up_sem,
    zsend_sem,
    zrecv_sem,
    hsend_sem,
    hrecv_sem,
    fsend_sem,
    frecv_sem,
    out_sem,
    passing,
    leg_sem,
):
    rows, rhs, wide = vin.shape
    block = wide // 2
    nonzero = mats.shape[1]
    chunks = rhs // CHUNK
    z = lax.axis_index("sweep")
    t = lax.axis_index("tile")
    has_left = t > 0
    has_right = t < tiles - 1
    has_above = z < sweeps - 1
    has_below = z > 0
    top = jnp.logical_not(has_above)
    far_left = has_left & (lax.rem(t, FAR_EVERY) == 0)
    far_right = has_right & (lax.rem(t, FAR_EVERY) == FAR_EVERY - 1)
    is_far = far_left | far_right
    is_a = t == tiles // 2 - 1
    is_b = t == tiles // 2
    is_pair = is_a | is_b
    via = (is_pair & top, ((t == 0) | (t == tiles - 1)) & top)
    send_left = has_left & (jnp.logical_not(far_left) | (top & jnp.logical_not(is_b)))
    send_right = has_right & (jnp.logical_not(far_right) | (top & jnp.logical_not(is_a)))
    left = jnp.maximum(t - 1, 0)
    right = jnp.minimum(t + 1, tiles - 1)
    below = jnp.maximum(z - 1, 0)
    above = jnp.minimum(z + 1, sweeps - 1)
    partner = jnp.where(far_left, left, right)
    partner_side = far_left.astype(jnp.int32)

    loads = [
        pltpu.make_async_copy(src_hbm, s_nat, load_sem.at[0]),
        pltpu.make_async_copy(thick_hbm, thick_ref, load_sem.at[1]),
        pltpu.make_async_copy(idx_hbm, idx_ref, load_sem.at[2]),
        pltpu.make_async_copy(fac_hbm, fac, load_sem.at[3]),
        pltpu.make_async_copy(fwd_hbm, f_nat, load_sem.at[4]),
    ]

    barrier = pltpu.get_barrier_semaphore()

    def greet(wanted, **device_id):
        @pl.when(wanted)
        def _():
            pl.semaphore_signal(barrier, inc=1, device_id=device_id)

    greet(is_far & has_above & jnp.logical_not(is_pair & (z == sweeps - 2)), sweep=above, tile=partner)
    between = jnp.where(is_a, 0, tiles - 1)
    beyond = jnp.where(t == 0, tiles // 2, tiles // 2 - 1)
    greet(via[1], tile=jnp.where(t == 0, tiles // 2 - 1, tiles // 2))
    greet(via[0], tile=jnp.where(is_a, tiles - 1, 0))
    greet(send_left, tile=left)
    greet(send_right, tile=right)
    greet(has_above, sweep=above)
    greet(is_far & has_below, sweep=below)

    for copy in loads:
        copy.start()

    def gain_rows(depth):
        thick = thick_ref[...]
        in_pml = (depth < thick) | (depth >= sweeps - thick)
        gain = jnp.where(in_pml, PML_FACTOR * LATERAL_WEIGHT, LATERAL_WEIGHT).astype(jnp.float32)
        return jnp.transpose(jnp.broadcast_to(gain, (block, rhs)), (1, 0))

    @pl.when(top)
    def _():
        vin[...] = jnp.zeros_like(vin)

    @pl.when(via[0])
    def _():
        hrecv[jnp.where(is_a, 1, 0), 0] = jnp.zeros(hrecv.shape[2:], hrecv.dtype)

    @pl.when(jnp.logical_not(has_left))
    def _():
        hrecv[0] = jnp.zeros(hrecv.shape[1:], hrecv.dtype)

    @pl.when(jnp.logical_not(has_right))
    def _():
        hrecv[1] = jnp.zeros(hrecv.shape[1:], hrecv.dtype)

    loads[1].wait()
    gq[...] = gain_rows(z)
    loads[0].wait()

    def turn_source(x, carry):
        for c in range(2):
            s_t[x, :, c * block : (c + 1) * block] = jnp.transpose(s_nat[c, 0, x], (1, 0))
        return carry

    lax.fori_loop(0, rows, turn_source, 0)

    def build(x, carry):
        for k in range(nonzero):
            re = fac[0, x, k, 0]
            im = fac[0, x, k, 1]
            re = jnp.transpose(re, (1, 0))
            im = jnp.transpose(im, (1, 0))
            mats[x, k, :block, :block] = re
            mats[x, k, :block, block:] = im
            mats[x, k, block:, :block] = -im
            mats[x, k, block:, block:] = re
        return carry

    one = [
        wanted.astype(jnp.int32)
        for wanted in (
            has_below,
            send_left,
            send_right,
            is_far & has_below & jnp.logical_not(via[0]),
            is_far & has_above,
            via[0],
            via[1],
        )
    ]
    pl.semaphore_wait(barrier, sum(one[1:], one[0]))

    lane = lax.broadcasted_iota(jnp.int32, (CHUNK, block), 1)
    left_on = has_left.astype(jnp.float32)
    right_on = has_right.astype(jnp.float32)

    def beside(v):
        up = jnp.where(lane == block - 1, 0.0, pltpu.roll(v, block - 1, 1))
        down = jnp.where(lane == 0, 0.0, pltpu.roll(v, 1, 1))
        return up + down

    hand_up = pltpu.make_async_remote_copy(
        src_ref=s_t.at[pl.ds(jnp.where(far_left, 0, rows - 2), 2)],
        dst_ref=s_next,
        send_sem=up_sem.at[0],
        recv_sem=up_sem.at[1],
        device_id={"sweep": above},
    )

    @pl.when(is_far & has_above)
    def _():
        hand_up.start()

    def span(g):
        return pl.ds(pl.multiple_of(g * CHUNK, CHUNK), CHUNK)

    def hand_down(g):
        return pltpu.make_async_remote_copy(
            src_ref=vout.at[:, span(g)],
            dst_ref=vin.at[:, span(g)],
            send_sem=zsend_sem.at[g],
            recv_sem=zrecv_sem.at[g],
            device_id={"sweep": below},
        )

    def to_left(g):
        return pltpu.make_async_remote_copy(
            src_ref=hsend.at[0, :, span(g)],
            dst_ref=hrecv.at[1, :, span(g)],
            send_sem=hsend_sem.at[0, g],
            recv_sem=hrecv_sem.at[1, g],
            device_id={"tile": left},
        )

    def to_right(g):
        return pltpu.make_async_remote_copy(
            src_ref=hsend.at[1, :, span(g)],
            dst_ref=hrecv.at[0, :, span(g)],
            send_sem=hsend_sem.at[1, g],
            recv_sem=hrecv_sem.at[0, g],
            device_id={"tile": right},
        )

    def to_partner(g):
        return pltpu.make_async_remote_copy(
            src_ref=fsend.at[:, span(g)],
            dst_ref=hrecv.at[partner_side, :, span(g)],
            send_sem=fsend_sem.at[g],
            recv_sem=frecv_sem.at[g],
            device_id={"sweep": below, "tile": partner},
        )

    def first_leg(g):
        return pltpu.make_async_remote_copy(
            src_ref=hsend.at[jnp.where(is_a, 1, 0), pl.ds(1, 2), span(g)],
            dst_ref=passing.at[:, span(g)],
            send_sem=leg_sem.at[0, g],
            recv_sem=leg_sem.at[1, g],
            device_id={"tile": between},
        )

    def second_leg(g):
        return pltpu.make_async_remote_copy(
            src_ref=passing.at[:, span(g)],
            dst_ref=hrecv.at[jnp.where(t == 0, 0, 1), pl.ds(1, 2), span(g)],
            send_sem=leg_sem.at[2, g],
            recv_sem=leg_sem.at[3, g],
            device_id={"tile": beyond},
        )

    def turned_half(h):
        return slice(h * block, (h + 1) * block)

    def keep(h):
        return pltpu.make_async_copy(
            o_nat.at[:, :, :, :, turned_half(h)],
            out_hbm.at[:, :, :, :, turned_half(h)],
            out_sem.at[h],
        )

    def finish(h):
        hs = turned_half(h)

        def one_row(x, carry):
            total = jnp.zeros((block, block), jnp.float32)
            for c in range(2):
                turned = jnp.transpose(vout[x, hs, c * block : (c + 1) * block], (1, 0))
                o_nat[c, 0, x, :, hs] = turned
                total = total + f_nat[c, 0, x, :, hs].astype(jnp.float32) * turned.astype(
                    jnp.float32
                )
            summed = jnp.sum(jnp.transpose(total, (1, 0)), axis=0, keepdims=True)
            if h > 0:
                summed = summed + grad[0, pl.ds(x, 1), :]
            if h == rhs // block - 1:
                summed = summed * (1.0 / math.sqrt(rhs))
            grad[0, pl.ds(x, 1), :] = summed
            return carry

        lax.fori_loop(0, rows, one_row, 0)
        keep(h).start()

    def edges_out(g):
        rs = span(g)

        @pl.when(has_above)
        def _():
            hand_down(g).wait_recv()

        scale = gq[rs, :]
        for c in range(2):
            ls = slice(c * block, (c + 1) * block)
            v = [vin[x, rs, ls].astype(jnp.float32) for x in range(rows)]
            for x in range(rows):
                total = beside(v[x])
                if x > 0:
                    total = total + v[x - 1]
                if x < rows - 1:
                    total = total + v[x + 1]
                w = s_t[x, rs, ls].astype(jnp.float32) - scale * total
                low = w.astype(jnp.bfloat16)
                if x == 0:
                    part[0, rs, ls] = w
                    hsend[0, 1, rs, ls] = low
                    hsend[0, 0, rs, ls] = vin[0, rs, ls]
                elif x == rows - 1:
                    part[1, rs, ls] = w
                    hsend[1, 1, rs, ls] = low
                    hsend[1, 0, rs, ls] = vin[rows - 1, rs, ls]
                else:
                    wext[2 + x, rs, ls] = low
                    if x == 1:
                        hsend[0, 2, rs, ls] = low
                    if x == rows - 2:
                        hsend[1, 2, rs, ls] = low

        @pl.when(send_left)
        def _():
            to_left(g).start()

        @pl.when(send_right)
        def _():
            to_right(g).start()

        @pl.when(via[0])
        def _():
            first_leg(g).start()

    def rows_out(g):
        rs = span(g)

        @pl.when(send_left)
        def _():
            to_right(g).wait_recv()

        @pl.when(send_right)
        def _():
            to_left(g).wait_recv()

        @pl.when(is_far & has_above)
        def _():
            to_partner(g).wait_recv()

        @pl.when(via[0])
        def _():
            second_leg(g).wait_recv()

        def settle():
            scale = gq[rs, :]
            for c in range(2):
                ls = slice(c * block, (c + 1) * block)
                near = hrecv[0, 0, rs, ls].astype(jnp.float32)
                wext[2, rs, ls] = (part[0, rs, ls] - scale * near).astype(jnp.bfloat16)
                near = hrecv[1, 0, rs, ls].astype(jnp.float32)
                wext[rows + 1, rs, ls] = (part[1, rs, ls] - scale * near).astype(jnp.bfloat16)
                mine = vin[0, rs, ls].astype(jnp.float32) * left_on
                wext[1, rs, ls] = (hrecv[0, 1, rs, ls].astype(jnp.float32) - scale * mine).astype(
                    jnp.bfloat16
                )
                mine = vin[rows - 1, rs, ls].astype(jnp.float32) * right_on
                wext[rows + 2, rs, ls] = (
                    hrecv[1, 1, rs, ls].astype(jnp.float32) - scale * mine
                ).astype(jnp.bfloat16)
                wext[0, rs, ls] = hrecv[0, 2, rs, ls]
                wext[rows + 3, rs, ls] = hrecv[1, 2, rs, ls]

        def field_row(x):
            acc = None
            for k in range(nonzero):
                term = jnp.dot(
                    wext[idx_ref[k, 0, x], rs, :],
                    mats[x, k],
                    preferred_element_type=jnp.float32,
                )
                acc = term if acc is None else acc + term
            row = acc.astype(jnp.bfloat16)
            vout[x, rs, :] = row
            return row

        def near_only():
            settle()
            for x in range(rows):
                field_row(x)

        def with_far(edge, inward):
            settle()
            v = [field_row(edge + i * inward) for i in range(3)]
            scale = gq_next[rs, :]
            first = 0 if inward > 0 else 1
            fsend[0, rs, :] = v[0]
            for c in range(2):
                ls = slice(c * block, (c + 1) * block)
                v0, v1, v2 = (row[:, ls].astype(jnp.float32) for row in v)
                source = s_next[first, rs, ls].astype(jnp.float32)
                fsend[1, rs, ls] = (source - scale * (v1 + beside(v0))).astype(jnp.bfloat16)
                source = s_next[1 - first, rs, ls].astype(jnp.float32)
                fsend[2, rs, ls] = (source - scale * (v0 + v2 + beside(v1))).astype(jnp.bfloat16)
            to_partner(g).start()
            for i in range(3, rows):
                field_row(edge + i * inward)

        @pl.when(far_left & has_below)
        def _():
            with_far(0, 1)

        @pl.when(far_right & has_below)
        def _():
            with_far(rows - 1, -1)

        @pl.when(jnp.logical_not(is_far & has_below))
        def _():
            near_only()

        @pl.when(has_below)
        def _():
            hand_down(g).start()

    def first_edges(g, carry):
        edges_out(g)
        return carry

    depth = jnp.where(is_far & (t != tiles // 2) & (t != tiles // 2 - 1), 1, DEPTH)
    ahead = jnp.where(top, chunks, depth)
    lax.fori_loop(0, jnp.where(top, chunks, 0), first_edges, 0)

    @pl.when(via[1])
    def _():
        def forward(g, carry):
            first_leg(g).wait_recv()
            second_leg(g).start()
            return carry

        lax.fori_loop(0, chunks, forward, 0)

    loads[3].wait()
    loads[2].wait()
    lax.fori_loop(0, rows, build, 0)

    @pl.when(is_far & has_below)
    def _():
        gq_next[...] = gain_rows(z - 1)
        hand_up.wait_recv()

    lax.fori_loop(0, jnp.where(top, 0, depth), first_edges, 0)

    def step(g, carry):
        @pl.when(g + ahead < chunks)
        def _():
            edges_out(g + ahead)

        rows_out(g)
        return carry

    halves = rhs // block
    per_half = chunks // halves
    for h in range(halves - 1):
        lax.fori_loop(h * per_half, (h + 1) * per_half, step, 0)

        @pl.when(jnp.logical_not(has_below))
        def _():
            loads[4].wait()
            finish(h)

    lax.fori_loop((halves - 1) * per_half, chunks, step, 0)

    @pl.when(has_below)
    def _():
        loads[4].wait()
        for h in range(halves - 1):
            finish(h)

    finish(halves - 1)
    grad_copy = pltpu.make_async_copy(grad, grad_hbm, out_sem.at[halves])
    grad_copy.start()


    @pl.when(is_far & has_above)
    def _():
        hand_up.wait_send()

    def drain(g, carry):
        @pl.when(has_below)
        def _():
            hand_down(g).wait_send()

        @pl.when(is_far & has_below)
        def _():
            to_partner(g).wait_send()

        @pl.when(send_left)
        def _():
            to_left(g).wait_send()

        @pl.when(send_right)
        def _():
            to_right(g).wait_send()

        @pl.when(via[0])
        def _():
            first_leg(g).wait_send()

        @pl.when(via[1])
        def _():
            second_leg(g).wait_send()

        return carry

    lax.fori_loop(0, chunks, drain, 0)
    for h in range(halves):
        keep(h).wait()
    grad_copy.wait()


def copy_kernel(adjoint_in, gradient_in, adjoint_out, gradient_out, held, held_gradient, sem):
    rows = adjoint_in.shape[2]
    pieces = [(gradient_in, held_gradient, gradient_out)]
    for c in range(2):
        for x in range(rows):
            pieces.append((adjoint_in.at[c, 0, x], held.at[c, x], adjoint_out.at[c, 0, x]))
    fetched = [
        pltpu.make_async_copy(source, here, sem.at[0, i])
        for i, (source, here, _) in enumerate(pieces)
    ]
    stored = [
        pltpu.make_async_copy(here, target, sem.at[1, i])
        for i, (_, here, target) in enumerate(pieces)
    ]
    for copy in fetched:
        copy.start()
    for fetch, store in zip(fetched, stored):
        fetch.wait()
        store.start()
    for copy in stored:
        copy.wait()


def on_device(sweeps, tiles, adjoint_source, forward_field, factor_blocks, factor_index, pml_thickness):
    _, layers, rows, block, rhs = adjoint_source.shape
    assert layers == 1
    nonzero = factor_blocks.shape[2]
    wide = 2 * block
    chunks = rhs // CHUNK
    bf16 = jnp.bfloat16
    f32 = jnp.float32
    hbm_spec = pl.BlockSpec(memory_space=pltpu.HBM)
    index = jnp.transpose(factor_index, (2, 0, 1))
    thickness = pml_thickness[None]
    outs = (
        jax.ShapeDtypeStruct(adjoint_source.shape, bf16),
        jax.ShapeDtypeStruct((1, rows, block), f32),
    )
    fields = pl.pallas_call(
        functools.partial(sweep_kernel, sweeps, tiles),
        out_shape=outs,
        in_specs=[hbm_spec] * 5,
        out_specs=(hbm_spec, hbm_spec),
        scratch_shapes=[
            pltpu.SMEM(index.shape, jnp.int32),
            pltpu.VMEM(thickness.shape, jnp.int32),
            pltpu.VMEM(adjoint_source.shape, bf16),
            pltpu.VMEM(forward_field.shape, bf16),
            pltpu.VMEM(adjoint_source.shape, bf16),
            pltpu.VMEM((1, rows, block), f32),
            pltpu.VMEM(factor_blocks.shape, bf16),
            pltpu.VMEM((rows, rhs, wide), bf16),
            pltpu.VMEM((2, rhs, wide), bf16),
            pltpu.VMEM((rhs, block), f32),
            pltpu.VMEM((rhs, block), f32),
            pltpu.VMEM((rows, nonzero, wide, wide), bf16),
            pltpu.VMEM((rows, rhs, wide), bf16),
            pltpu.VMEM((rows, rhs, wide), bf16),
            pltpu.VMEM((2, rhs, wide), f32),
            pltpu.VMEM((rows + 4, rhs, wide), bf16),
            pltpu.VMEM((2, 3, rhs, wide), bf16),
            pltpu.VMEM((3, rhs, wide), bf16),
            pltpu.VMEM((2, 3, rhs, wide), bf16),
            pltpu.SemaphoreType.DMA((5,)),
            pltpu.SemaphoreType.DMA((2,)),
            pltpu.SemaphoreType.DMA((chunks,)),
            pltpu.SemaphoreType.DMA((chunks,)),
            pltpu.SemaphoreType.DMA((2, chunks)),
            pltpu.SemaphoreType.DMA((2, chunks)),
            pltpu.SemaphoreType.DMA((chunks,)),
            pltpu.SemaphoreType.DMA((chunks,)),
            pltpu.SemaphoreType.DMA((rhs // block + 1,)),
            pltpu.VMEM((2, rhs, wide), bf16),
            pltpu.SemaphoreType.DMA((4, chunks)),
        ],
        compiler_params=pltpu.CompilerParams(
            collective_id=0, has_side_effects=True, vmem_limit_bytes=63 * 1024 * 1024
        ),
    )(index, thickness, adjoint_source, factor_blocks, forward_field)
    return pl.pallas_call(
        copy_kernel,
        out_shape=outs,
        in_specs=[hbm_spec] * 2,
        out_specs=(hbm_spec, hbm_spec),
        scratch_shapes=[
            pltpu.VMEM((2, rows, block, rhs), bf16),
            pltpu.VMEM((1, rows, block), f32),
            pltpu.SemaphoreType.DMA((2, 2 * rows + 1)),
        ],
    )(*fields)


def solution(mesh):
    placed = (
        P(None, "sweep", "tile", None, None),
        P(None, "sweep", "tile", None, None),
        P("sweep", "tile", None, None, None, None),
        P("sweep", "tile", None),
        P(),
    )
    return jax.shard_map(
        functools.partial(on_device, mesh.shape["sweep"], mesh.shape["tile"]),
        mesh=mesh,
        in_specs=placed,
        out_specs=(P(None, "sweep", "tile", None, None), P("sweep", "tile", None)),
        check_vma=False,
    )
```

```python
import functools
import math

import jax
import jax.numpy as jnp
from jax import lax
from jax.experimental import pallas as pl
from jax.experimental.pallas import tpu as pltpu
from jax.sharding import PartitionSpec as P

PML_FACTOR = 0.55
LATERAL_WEIGHT = 0.25
CHUNK = 32
DEPTH = 2
FAR_EVERY = 8


def sweep_kernel(
    sweeps,
    tiles,
    idx_hbm,
    thick_hbm,
    src_hbm,
    fac_hbm,
    fwd_hbm,
    o_nat,
    grad,
    idx_ref,
    thick_ref,
    s_nat,
    f_nat,
    fac,
    s_t,
    s_next,
    gq,
    gq_next,
    mats,
    vin,
    vout,
    part,
    wext,
    hsend,
    fsend,
    hrecv,
    load_sem,
    up_sem,
    zsend_sem,
    zrecv_sem,
    hsend_sem,
    hrecv_sem,
    fsend_sem,
    frecv_sem,
    passing,
    leg_sem,
):
    chunks, rows, _, wide = vin.shape
    rhs = chunks * CHUNK
    block = wide // 2
    nonzero = mats.shape[1]
    z = lax.axis_index("sweep")
    t = lax.axis_index("tile")
    has_left = t > 0
    has_right = t < tiles - 1
    has_above = z < sweeps - 1
    has_below = z > 0
    top = jnp.logical_not(has_above)
    far_left = has_left & (lax.rem(t, FAR_EVERY) == 0)
    far_right = has_right & (lax.rem(t, FAR_EVERY) == FAR_EVERY - 1)
    is_far = far_left | far_right
    is_a = t == tiles // 2 - 1
    is_b = t == tiles // 2
    is_pair = is_a | is_b
    via = (is_pair & top, ((t == 0) | (t == tiles - 1)) & top)
    send_left = has_left & (jnp.logical_not(far_left) | (top & jnp.logical_not(is_b)))
    send_right = has_right & (jnp.logical_not(far_right) | (top & jnp.logical_not(is_a)))
    left = jnp.maximum(t - 1, 0)
    right = jnp.minimum(t + 1, tiles - 1)
    below = jnp.maximum(z - 1, 0)
    above = jnp.minimum(z + 1, sweeps - 1)
    partner = jnp.where(far_left, left, right)
    partner_side = far_left.astype(jnp.int32)

    loads = [
        pltpu.make_async_copy(src_hbm, s_nat, load_sem.at[0]),
        pltpu.make_async_copy(thick_hbm, thick_ref, load_sem.at[1]),
        pltpu.make_async_copy(idx_hbm, idx_ref, load_sem.at[2]),
        pltpu.make_async_copy(fac_hbm, fac, load_sem.at[3]),
        pltpu.make_async_copy(fwd_hbm, f_nat, load_sem.at[4]),
    ]

    barrier = pltpu.get_barrier_semaphore()

    def greet(wanted, **device_id):
        @pl.when(wanted)
        def _():
            pl.semaphore_signal(barrier, inc=1, device_id=device_id)

    greet(is_far & has_above & jnp.logical_not(is_pair & (z == sweeps - 2)), sweep=above, tile=partner)
    between = jnp.where(is_a, 0, tiles - 1)
    beyond = jnp.where(t == 0, tiles // 2, tiles // 2 - 1)
    greet(via[1], tile=jnp.where(t == 0, tiles // 2 - 1, tiles // 2))
    greet(via[0], tile=jnp.where(is_a, tiles - 1, 0))
    greet(send_left, tile=left)
    greet(send_right, tile=right)
    greet(has_above, sweep=above)
    greet(is_far & has_below, sweep=below)

    for copy in loads:
        copy.start()

    def gain_rows(depth):
        thick = thick_ref[...]
        in_pml = (depth < thick) | (depth >= sweeps - thick)
        gain = jnp.where(in_pml, PML_FACTOR * LATERAL_WEIGHT, LATERAL_WEIGHT).astype(jnp.float32)
        return jnp.transpose(jnp.broadcast_to(gain, (block, rhs)), (1, 0))

    @pl.when(top)
    def _():
        vin[...] = jnp.zeros_like(vin)

    @pl.when(via[0])
    def _():
        hrecv[:, jnp.where(is_a, 1, 0), 0] = jnp.zeros((chunks,) + hrecv.shape[3:], hrecv.dtype)

    @pl.when(jnp.logical_not(has_left))
    def _():
        hrecv[:, 0] = jnp.zeros((chunks,) + hrecv.shape[2:], hrecv.dtype)

    @pl.when(jnp.logical_not(has_right))
    def _():
        hrecv[:, 1] = jnp.zeros((chunks,) + hrecv.shape[2:], hrecv.dtype)

    loads[1].wait()
    gq[...] = gain_rows(z)
    loads[0].wait()

    def turn_source(x, carry):
        for c in range(2):
            s_t[x, :, c * block : (c + 1) * block] = jnp.transpose(s_nat[c, 0, x], (1, 0))
        return carry

    lax.fori_loop(0, rows, turn_source, 0)

    def build(x, carry):
        for k in range(nonzero):
            re = fac[0, x, k, 0]
            im = fac[0, x, k, 1]
            re = jnp.transpose(re, (1, 0))
            im = jnp.transpose(im, (1, 0))
            mats[x, k, :block, :block] = re
            mats[x, k, :block, block:] = im
            mats[x, k, block:, :block] = -im
            mats[x, k, block:, block:] = re
        return carry

    one = [
        wanted.astype(jnp.int32)
        for wanted in (
            has_below,
            send_left,
            send_right,
            is_far & has_below & jnp.logical_not(via[0]),
            is_far & has_above,
            via[0],
            via[1],
        )
    ]
    pl.semaphore_wait(barrier, sum(one[1:], one[0]))

    lane = lax.broadcasted_iota(jnp.int32, (CHUNK, block), 1)
    left_on = has_left.astype(jnp.float32)
    right_on = has_right.astype(jnp.float32)

    def beside(v):
        up = jnp.where(lane == block - 1, 0.0, pltpu.roll(v, block - 1, 1))
        down = jnp.where(lane == 0, 0.0, pltpu.roll(v, 1, 1))
        return up + down

    hand_up = pltpu.make_async_remote_copy(
        src_ref=s_t.at[pl.ds(jnp.where(far_left, 0, rows - 2), 2)],
        dst_ref=s_next,
        send_sem=up_sem.at[0],
        recv_sem=up_sem.at[1],
        device_id={"sweep": above},
    )

    @pl.when(is_far & has_above)
    def _():
        hand_up.start()

    def span(g):
        return pl.ds(pl.multiple_of(g * CHUNK, CHUNK), CHUNK)

    def hand_down(g):
        return pltpu.make_async_remote_copy(
            src_ref=vout.at[g],
            dst_ref=vin.at[g],
            send_sem=zsend_sem.at[g],
            recv_sem=zrecv_sem.at[g],
            device_id={"sweep": below},
        )

    def to_left(g):
        return pltpu.make_async_remote_copy(
            src_ref=hsend.at[g, 0],
            dst_ref=hrecv.at[g, 1],
            send_sem=hsend_sem.at[0, g],
            recv_sem=hrecv_sem.at[1, g],
            device_id={"tile": left},
        )

    def to_right(g):
        return pltpu.make_async_remote_copy(
            src_ref=hsend.at[g, 1],
            dst_ref=hrecv.at[g, 0],
            send_sem=hsend_sem.at[1, g],
            recv_sem=hrecv_sem.at[0, g],
            device_id={"tile": right},
        )

    def to_partner(g):
        return pltpu.make_async_remote_copy(
            src_ref=fsend.at[g],
            dst_ref=hrecv.at[g, partner_side],
            send_sem=fsend_sem.at[g],
            recv_sem=frecv_sem.at[g],
            device_id={"sweep": below, "tile": partner},
        )

    def first_leg(g):
        return pltpu.make_async_remote_copy(
            src_ref=hsend.at[g, jnp.where(is_a, 1, 0), pl.ds(1, 2)],
            dst_ref=passing.at[g],
            send_sem=leg_sem.at[0, g],
            recv_sem=leg_sem.at[1, g],
            device_id={"tile": between},
        )

    def second_leg(g):
        return pltpu.make_async_remote_copy(
            src_ref=passing.at[g],
            dst_ref=hrecv.at[g, jnp.where(t == 0, 0, 1), pl.ds(1, 2)],
            send_sem=leg_sem.at[2, g],
            recv_sem=leg_sem.at[3, g],
            device_id={"tile": beyond},
        )

    def turned_half(h):
        return slice(h * block, (h + 1) * block)

    def finish(h):
        hs = turned_half(h)

        def one_row(x, carry):
            total = jnp.zeros((block, block), jnp.float32)
            for c in range(2):
                first = h * (block // CHUNK)
                field = vout[first : first + block // CHUNK, x, :, c * block : (c + 1) * block]
                turned = jnp.transpose(field.reshape(block, block), (1, 0))
                o_nat[c, 0, x, :, hs] = turned
                total = total + f_nat[c, 0, x, :, hs].astype(jnp.float32) * turned.astype(
                    jnp.float32
                )
            summed = jnp.sum(jnp.transpose(total, (1, 0)), axis=0, keepdims=True)
            if h > 0:
                summed = summed + grad[0, pl.ds(x, 1), :]
            if h == rhs // block - 1:
                summed = summed * (1.0 / math.sqrt(rhs))
            grad[0, pl.ds(x, 1), :] = summed
            return carry

        lax.fori_loop(0, rows, one_row, 0)

    def edges_out(g):
        rs = span(g)

        @pl.when(has_above)
        def _():
            hand_down(g).wait_recv()

        scale = gq[rs, :]
        for c in range(2):
            ls = slice(c * block, (c + 1) * block)
            v = [vin[g, x, :, ls].astype(jnp.float32) for x in range(rows)]
            for x in range(rows):
                total = beside(v[x])
                if x > 0:
                    total = total + v[x - 1]
                if x < rows - 1:
                    total = total + v[x + 1]
                w = s_t[x, rs, ls].astype(jnp.float32) - scale * total
                low = w.astype(jnp.bfloat16)
                if x == 0:
                    part[0, rs, ls] = w
                    hsend[g, 0, 1, :, ls] = low
                    hsend[g, 0, 0, :, ls] = vin[g, 0, :, ls]
                elif x == rows - 1:
                    part[1, rs, ls] = w
                    hsend[g, 1, 1, :, ls] = low
                    hsend[g, 1, 0, :, ls] = vin[g, rows - 1, :, ls]
                else:
                    wext[2 + x, rs, ls] = low
                    if x == 1:
                        hsend[g, 0, 2, :, ls] = low
                    if x == rows - 2:
                        hsend[g, 1, 2, :, ls] = low

        @pl.when(send_left)
        def _():
            to_left(g).start()

        @pl.when(send_right)
        def _():
            to_right(g).start()

        @pl.when(via[0])
        def _():
            first_leg(g).start()

    def rows_out(g):
        rs = span(g)

        @pl.when(send_left)
        def _():
            to_right(g).wait_recv()

        @pl.when(send_right)
        def _():
            to_left(g).wait_recv()

        @pl.when(is_far & has_above)
        def _():
            to_partner(g).wait_recv()

        @pl.when(via[0])
        def _():
            second_leg(g).wait_recv()

        def settle():
            scale = gq[rs, :]
            for c in range(2):
                ls = slice(c * block, (c + 1) * block)
                near = hrecv[g, 0, 0, :, ls].astype(jnp.float32)
                wext[2, rs, ls] = (part[0, rs, ls] - scale * near).astype(jnp.bfloat16)
                near = hrecv[g, 1, 0, :, ls].astype(jnp.float32)
                wext[rows + 1, rs, ls] = (part[1, rs, ls] - scale * near).astype(jnp.bfloat16)
                mine = vin[g, 0, :, ls].astype(jnp.float32) * left_on
                wext[1, rs, ls] = (hrecv[g, 0, 1, :, ls].astype(jnp.float32) - scale * mine).astype(
                    jnp.bfloat16
                )
                mine = vin[g, rows - 1, :, ls].astype(jnp.float32) * right_on
                wext[rows + 2, rs, ls] = (
                    hrecv[g, 1, 1, :, ls].astype(jnp.float32) - scale * mine
                ).astype(jnp.bfloat16)
                wext[0, rs, ls] = hrecv[g, 0, 2, :, ls]
                wext[rows + 3, rs, ls] = hrecv[g, 1, 2, :, ls]

        def field_row(x):
            acc = None
            for k in range(nonzero):
                term = jnp.dot(
                    wext[idx_ref[k, 0, x], rs, :],
                    mats[x, k],
                    preferred_element_type=jnp.float32,
                )
                acc = term if acc is None else acc + term
            row = acc.astype(jnp.bfloat16)
            vout[g, x, :, :] = row
            return row

        def near_only():
            settle()
            for x in range(rows):
                field_row(x)

        def with_far(edge, inward):
            settle()
            v = [field_row(edge + i * inward) for i in range(3)]
            scale = gq_next[rs, :]
            first = 0 if inward > 0 else 1
            fsend[g, 0, :, :] = v[0]
            for c in range(2):
                ls = slice(c * block, (c + 1) * block)
                v0, v1, v2 = (row[:, ls].astype(jnp.float32) for row in v)
                source = s_next[first, rs, ls].astype(jnp.float32)
                fsend[g, 1, :, ls] = (source - scale * (v1 + beside(v0))).astype(jnp.bfloat16)
                source = s_next[1 - first, rs, ls].astype(jnp.float32)
                fsend[g, 2, :, ls] = (source - scale * (v0 + v2 + beside(v1))).astype(jnp.bfloat16)
            for i in range(3, rows):
                field_row(edge + i * inward)
            to_partner(g).start()

        @pl.when(far_left & has_below)
        def _():
            with_far(0, 1)

        @pl.when(far_right & has_below)
        def _():
            with_far(rows - 1, -1)

        @pl.when(jnp.logical_not(is_far & has_below))
        def _():
            near_only()

        @pl.when(has_below)
        def _():
            hand_down(g).start()

    def first_edges(g, carry):
        edges_out(g)
        return carry

    depth = jnp.where(is_pair, 2, jnp.where(is_far, 0, 2))
    ahead = jnp.where(top, chunks, depth)
    lax.fori_loop(0, jnp.where(top, chunks, 0), first_edges, 0)

    @pl.when(via[1])
    def _():
        def forward(g, carry):
            first_leg(g).wait_recv()
            second_leg(g).start()
            return carry

        lax.fori_loop(0, chunks, forward, 0)

    loads[3].wait()
    loads[2].wait()
    lax.fori_loop(0, rows, build, 0)

    @pl.when(is_far & has_below)
    def _():
        gq_next[...] = gain_rows(z - 1)
        hand_up.wait_recv()

    lax.fori_loop(0, jnp.where(top, 0, depth), first_edges, 0)

    def step(g, carry):
        @pl.when(g + ahead < chunks)
        def _():
            edges_out(g + ahead)

        rows_out(g)
        return carry

    halves = rhs // block
    per_half = chunks // halves
    for h in range(halves - 1):
        lax.fori_loop(h * per_half, (h + 1) * per_half, step, 0)

        @pl.when(jnp.logical_not(has_below))
        def _():
            loads[4].wait()
            finish(h)

    lax.fori_loop((halves - 1) * per_half, chunks, step, 0)

    @pl.when(has_below)
    def _():
        loads[4].wait()
        for h in range(halves - 1):
            finish(h)

    finish(halves - 1)


    @pl.when(is_far & has_above)
    def _():
        hand_up.wait_send()

    def drain(g, carry):
        @pl.when(has_below)
        def _():
            hand_down(g).wait_send()

        @pl.when(is_far & has_below)
        def _():
            to_partner(g).wait_send()

        @pl.when(send_left)
        def _():
            to_left(g).wait_send()

        @pl.when(send_right)
        def _():
            to_right(g).wait_send()

        @pl.when(via[0])
        def _():
            first_leg(g).wait_send()

        @pl.when(via[1])
        def _():
            second_leg(g).wait_send()

        return carry

    lax.fori_loop(0, chunks, drain, 0)


def copy_kernel(adjoint_in, gradient_in, adjoint_out, gradient_out, sem):
    rows = adjoint_in.shape[2]
    copies = [pltpu.make_async_copy(gradient_in, gradient_out, sem.at[2 * rows])]
    for c in range(2):
        for x in range(rows):
            copies.append(
                pltpu.make_async_copy(
                    adjoint_in.at[c, 0, x], adjoint_out.at[c, 0, x], sem.at[c * rows + x]
                )
            )
    for copy in copies:
        copy.start()
    for copy in copies:
        copy.wait()


def on_device(sweeps, tiles, adjoint_source, forward_field, factor_blocks, factor_index, pml_thickness):
    _, layers, rows, block, rhs = adjoint_source.shape
    assert layers == 1
    nonzero = factor_blocks.shape[2]
    wide = 2 * block
    chunks = rhs // CHUNK
    bf16 = jnp.bfloat16
    f32 = jnp.float32
    hbm_spec = pl.BlockSpec(memory_space=pltpu.HBM)
    vmem_spec = pl.BlockSpec(memory_space=pltpu.VMEM)
    index = jnp.transpose(factor_index, (2, 0, 1))
    thickness = pml_thickness[None]
    outs = (
        jax.ShapeDtypeStruct(adjoint_source.shape, bf16),
        jax.ShapeDtypeStruct((1, rows, block), f32),
    )
    fields = pl.pallas_call(
        functools.partial(sweep_kernel, sweeps, tiles),
        out_shape=outs,
        in_specs=[hbm_spec] * 5,
        out_specs=(vmem_spec, vmem_spec),
        scratch_shapes=[
            pltpu.SMEM(index.shape, jnp.int32),
            pltpu.VMEM(thickness.shape, jnp.int32),
            pltpu.VMEM(adjoint_source.shape, bf16),
            pltpu.VMEM(forward_field.shape, bf16),
            pltpu.VMEM(factor_blocks.shape, bf16),
            pltpu.VMEM((rows, rhs, wide), bf16),
            pltpu.VMEM((2, rhs, wide), bf16),
            pltpu.VMEM((rhs, block), f32),
            pltpu.VMEM((rhs, block), f32),
            pltpu.VMEM((rows, nonzero, wide, wide), bf16),
            pltpu.VMEM((chunks, rows, CHUNK, wide), bf16),
            pltpu.VMEM((chunks, rows, CHUNK, wide), bf16),
            pltpu.VMEM((2, rhs, wide), f32),
            pltpu.VMEM((rows + 4, rhs, wide), bf16),
            pltpu.VMEM((chunks, 2, 3, CHUNK, wide), bf16),
            pltpu.VMEM((chunks, 3, CHUNK, wide), bf16),
            pltpu.VMEM((chunks, 2, 3, CHUNK, wide), bf16),
            pltpu.SemaphoreType.DMA((5,)),
            pltpu.SemaphoreType.DMA((2,)),
            pltpu.SemaphoreType.DMA((chunks,)),
            pltpu.SemaphoreType.DMA((chunks,)),
            pltpu.SemaphoreType.DMA((2, chunks)),
            pltpu.SemaphoreType.DMA((2, chunks)),
            pltpu.SemaphoreType.DMA((chunks,)),
            pltpu.SemaphoreType.DMA((chunks,)),
            pltpu.VMEM((chunks, 2, CHUNK, wide), bf16),
            pltpu.SemaphoreType.DMA((4, chunks)),
        ],
        compiler_params=pltpu.CompilerParams(
            collective_id=0, has_side_effects=True, vmem_limit_bytes=32 * 1024 * 1024
        ),
    )(*(
        pltpu.with_memory_space_constraint(operand, pltpu.HBM)
        for operand in (index, thickness, adjoint_source, factor_blocks, forward_field)
    ))
    return pl.pallas_call(
        copy_kernel,
        out_shape=outs,
        in_specs=[vmem_spec] * 2,
        out_specs=(hbm_spec, hbm_spec),
        scratch_shapes=[pltpu.SemaphoreType.DMA((2 * rows + 1,))],
        compiler_params=pltpu.CompilerParams(vmem_limit_bytes=4 * 1024 * 1024),
    )(*fields)


def solution(mesh):
    placed = (
        P(None, "sweep", "tile", None, None),
        P(None, "sweep", "tile", None, None),
        P("sweep", "tile", None, None, None, None),
        P("sweep", "tile", None),
        P(),
    )
    return jax.shard_map(
        functools.partial(on_device, mesh.shape["sweep"], mesh.shape["tile"]),
        mesh=mesh,
        in_specs=placed,
        out_specs=(P(None, "sweep", "tile", None, None), P("sweep", "tile", None)),
        check_vma=False,
    )
```

```python
import functools
import math

import jax
import jax.numpy as jnp
from jax import lax
from jax.experimental import pallas as pl
from jax.experimental.pallas import tpu as pltpu
from jax.sharding import PartitionSpec as P

PML_FACTOR = 0.55
LATERAL_WEIGHT = 0.25
CHUNK = 32
DEPTH = 2
FAR_EVERY = 8


def sweep_kernel(
    sweeps,
    tiles,
    idx_hbm,
    thick_hbm,
    src_hbm,
    fac_hbm,
    fwd_hbm,
    o_nat,
    grad,
    idx_ref,
    thick_ref,
    s_nat,
    f_nat,
    fac,
    s_t,
    s_next,
    gq,
    gq_next,
    mats,
    vin,
    vout,
    part,
    wext,
    hsend,
    fsend,
    hrecv,
    load_sem,
    up_sem,
    zsend_sem,
    zrecv_sem,
    hsend_sem,
    hrecv_sem,
    fsend_sem,
    frecv_sem,
    passing,
    leg_sem,
):
    chunks, rows, _, wide = vin.shape
    rhs = chunks * CHUNK
    block = wide // 2
    nonzero = mats.shape[1]
    z = lax.axis_index("sweep")
    t = lax.axis_index("tile")
    has_left = t > 0
    has_right = t < tiles - 1
    has_above = z < sweeps - 1
    has_below = z > 0
    top = jnp.logical_not(has_above)
    far_left = has_left & (lax.rem(t, FAR_EVERY) == 0)
    far_right = has_right & (lax.rem(t, FAR_EVERY) == FAR_EVERY - 1)
    is_far = far_left | far_right
    is_a = t == tiles // 2 - 1
    is_b = t == tiles // 2
    is_pair = is_a | is_b
    via = (is_pair & top, ((t == 0) | (t == tiles - 1)) & top)
    send_left = has_left & (jnp.logical_not(far_left) | (top & jnp.logical_not(is_b)))
    send_right = has_right & (jnp.logical_not(far_right) | (top & jnp.logical_not(is_a)))
    left = jnp.maximum(t - 1, 0)
    right = jnp.minimum(t + 1, tiles - 1)
    below = jnp.maximum(z - 1, 0)
    above = jnp.minimum(z + 1, sweeps - 1)
    partner = jnp.where(far_left, left, right)
    partner_side = far_left.astype(jnp.int32)

    loads = [
        pltpu.make_async_copy(src_hbm, s_nat, load_sem.at[0]),
        pltpu.make_async_copy(thick_hbm, thick_ref, load_sem.at[1]),
        pltpu.make_async_copy(idx_hbm, idx_ref, load_sem.at[2]),
        pltpu.make_async_copy(fac_hbm, fac, load_sem.at[3]),
        pltpu.make_async_copy(fwd_hbm, f_nat, load_sem.at[4]),
    ]

    barrier = pltpu.get_barrier_semaphore()

    def greet(wanted, **device_id):
        @pl.when(wanted)
        def _():
            pl.semaphore_signal(barrier, inc=1, device_id=device_id)

    greet(is_far & has_above & jnp.logical_not(is_pair & (z == sweeps - 2)), sweep=above, tile=partner)
    between = jnp.where(is_a, 0, tiles - 1)
    beyond = jnp.where(t == 0, tiles // 2, tiles // 2 - 1)
    greet(via[1], tile=jnp.where(t == 0, tiles // 2 - 1, tiles // 2))
    greet(via[0], tile=jnp.where(is_a, tiles - 1, 0))
    greet(send_left, tile=left)
    greet(send_right, tile=right)
    greet(has_above, sweep=above)
    greet(is_far & has_below, sweep=below)

    for copy in loads:
        copy.start()

    def gain_rows(depth):
        thick = thick_ref[...]
        in_pml = (depth < thick) | (depth >= sweeps - thick)
        gain = jnp.where(in_pml, PML_FACTOR * LATERAL_WEIGHT, LATERAL_WEIGHT).astype(jnp.float32)
        return jnp.transpose(jnp.broadcast_to(gain, (block, rhs)), (1, 0))

    @pl.when(top)
    def _():
        vin[...] = jnp.zeros_like(vin)

    @pl.when(via[0])
    def _():
        hrecv[:, jnp.where(is_a, 1, 0), 0] = jnp.zeros((chunks,) + hrecv.shape[3:], hrecv.dtype)

    @pl.when(jnp.logical_not(has_left))
    def _():
        hrecv[:, 0] = jnp.zeros((chunks,) + hrecv.shape[2:], hrecv.dtype)

    @pl.when(jnp.logical_not(has_right))
    def _():
        hrecv[:, 1] = jnp.zeros((chunks,) + hrecv.shape[2:], hrecv.dtype)

    loads[1].wait()
    gq[...] = gain_rows(z)
    loads[0].wait()

    def turn_source(x, carry):
        for c in range(2):
            s_t[x, :, c * block : (c + 1) * block] = jnp.transpose(s_nat[c, 0, x], (1, 0))
        return carry

    lax.fori_loop(0, rows, turn_source, 0)

    def build(x, carry):
        for k in range(nonzero):
            re = fac[0, x, k, 0]
            im = fac[0, x, k, 1]
            re = jnp.transpose(re, (1, 0))
            im = jnp.transpose(im, (1, 0))
            mats[x, k, :block, :block] = re
            mats[x, k, :block, block:] = im
            mats[x, k, block:, :block] = -im
            mats[x, k, block:, block:] = re
        return carry

    one = [
        wanted.astype(jnp.int32)
        for wanted in (
            has_below,
            send_left,
            send_right,
            is_far & has_below & jnp.logical_not(via[0]),
            is_far & has_above,
            via[0],
            via[1],
        )
    ]
    pl.semaphore_wait(barrier, sum(one[1:], one[0]))

    lane = lax.broadcasted_iota(jnp.int32, (CHUNK, block), 1)
    left_on = has_left.astype(jnp.float32)
    right_on = has_right.astype(jnp.float32)

    def beside(v):
        up = jnp.where(lane == block - 1, 0.0, pltpu.roll(v, block - 1, 1))
        down = jnp.where(lane == 0, 0.0, pltpu.roll(v, 1, 1))
        return up + down

    hand_up = pltpu.make_async_remote_copy(
        src_ref=s_t.at[pl.ds(jnp.where(far_left, 0, rows - 2), 2)],
        dst_ref=s_next,
        send_sem=up_sem.at[0],
        recv_sem=up_sem.at[1],
        device_id={"sweep": above},
    )

    @pl.when(is_far & has_above)
    def _():
        hand_up.start()

    def span(g):
        return pl.ds(pl.multiple_of(g * CHUNK, CHUNK), CHUNK)

    def hand_down(g, half):
        some = pl.ds(half * (rows // 2), rows // 2)
        return pltpu.make_async_remote_copy(
            src_ref=vout.at[g, some],
            dst_ref=vin.at[g, some],
            send_sem=zsend_sem.at[half, g],
            recv_sem=zrecv_sem.at[half, g],
            device_id={"sweep": below},
        )

    def to_left(g):
        return pltpu.make_async_remote_copy(
            src_ref=hsend.at[g, 0],
            dst_ref=hrecv.at[g, 1],
            send_sem=hsend_sem.at[0, g],
            recv_sem=hrecv_sem.at[1, g],
            device_id={"tile": left},
        )

    def to_right(g):
        return pltpu.make_async_remote_copy(
            src_ref=hsend.at[g, 1],
            dst_ref=hrecv.at[g, 0],
            send_sem=hsend_sem.at[1, g],
            recv_sem=hrecv_sem.at[0, g],
            device_id={"tile": right},
        )

    def to_partner(g):
        return pltpu.make_async_remote_copy(
            src_ref=fsend.at[g],
            dst_ref=hrecv.at[g, partner_side],
            send_sem=fsend_sem.at[g],
            recv_sem=frecv_sem.at[g],
            device_id={"sweep": below, "tile": partner},
        )

    def first_leg(g):
        return pltpu.make_async_remote_copy(
            src_ref=hsend.at[g, jnp.where(is_a, 1, 0), pl.ds(1, 2)],
            dst_ref=passing.at[g],
            send_sem=leg_sem.at[0, g],
            recv_sem=leg_sem.at[1, g],
            device_id={"tile": between},
        )

    def second_leg(g):
        return pltpu.make_async_remote_copy(
            src_ref=passing.at[g],
            dst_ref=hrecv.at[g, jnp.where(t == 0, 0, 1), pl.ds(1, 2)],
            send_sem=leg_sem.at[2, g],
            recv_sem=leg_sem.at[3, g],
            device_id={"tile": beyond},
        )

    def turned_half(h):
        return slice(h * block, (h + 1) * block)

    def finish(h):
        hs = turned_half(h)

        def one_row(x, carry):
            total = jnp.zeros((block, block), jnp.float32)
            for c in range(2):
                first = h * (block // CHUNK)
                field = vout[first : first + block // CHUNK, x, :, c * block : (c + 1) * block]
                turned = jnp.transpose(field.reshape(block, block), (1, 0))
                o_nat[c, 0, x, :, hs] = turned
                total = total + f_nat[c, 0, x, :, hs].astype(jnp.float32) * turned.astype(
                    jnp.float32
                )
            summed = jnp.sum(jnp.transpose(total, (1, 0)), axis=0, keepdims=True)
            if h > 0:
                summed = summed + grad[0, pl.ds(x, 1), :]
            if h == rhs // block - 1:
                summed = summed * (1.0 / math.sqrt(rhs))
            grad[0, pl.ds(x, 1), :] = summed
            return carry

        lax.fori_loop(0, rows, one_row, 0)

    def edges_out(g):
        rs = span(g)

        @pl.when(has_above)
        def _():
            hand_down(g, 0).wait_recv()
            hand_down(g, 1).wait_recv()

        scale = gq[rs, :]
        for c in range(2):
            ls = slice(c * block, (c + 1) * block)
            v = [vin[g, x, :, ls].astype(jnp.float32) for x in range(rows)]
            for x in range(rows):
                total = beside(v[x])
                if x > 0:
                    total = total + v[x - 1]
                if x < rows - 1:
                    total = total + v[x + 1]
                w = s_t[x, rs, ls].astype(jnp.float32) - scale * total
                low = w.astype(jnp.bfloat16)
                if x == 0:
                    part[0, rs, ls] = w
                    hsend[g, 0, 1, :, ls] = low
                    hsend[g, 0, 0, :, ls] = vin[g, 0, :, ls]
                elif x == rows - 1:
                    part[1, rs, ls] = w
                    hsend[g, 1, 1, :, ls] = low
                    hsend[g, 1, 0, :, ls] = vin[g, rows - 1, :, ls]
                else:
                    wext[2 + x, rs, ls] = low
                    if x == 1:
                        hsend[g, 0, 2, :, ls] = low
                    if x == rows - 2:
                        hsend[g, 1, 2, :, ls] = low

        @pl.when(send_left)
        def _():
            to_left(g).start()

        @pl.when(send_right)
        def _():
            to_right(g).start()

        @pl.when(via[0])
        def _():
            first_leg(g).start()

    def rows_out(g):
        rs = span(g)

        @pl.when(send_left)
        def _():
            to_right(g).wait_recv()

        @pl.when(send_right)
        def _():
            to_left(g).wait_recv()

        @pl.when(is_far & has_above)
        def _():
            to_partner(g).wait_recv()

        @pl.when(via[0])
        def _():
            second_leg(g).wait_recv()

        def settle():
            scale = gq[rs, :]
            for c in range(2):
                ls = slice(c * block, (c + 1) * block)
                near = hrecv[g, 0, 0, :, ls].astype(jnp.float32)
                wext[2, rs, ls] = (part[0, rs, ls] - scale * near).astype(jnp.bfloat16)
                near = hrecv[g, 1, 0, :, ls].astype(jnp.float32)
                wext[rows + 1, rs, ls] = (part[1, rs, ls] - scale * near).astype(jnp.bfloat16)
                mine = vin[g, 0, :, ls].astype(jnp.float32) * left_on
                wext[1, rs, ls] = (hrecv[g, 0, 1, :, ls].astype(jnp.float32) - scale * mine).astype(
                    jnp.bfloat16
                )
                mine = vin[g, rows - 1, :, ls].astype(jnp.float32) * right_on
                wext[rows + 2, rs, ls] = (
                    hrecv[g, 1, 1, :, ls].astype(jnp.float32) - scale * mine
                ).astype(jnp.bfloat16)
                wext[0, rs, ls] = hrecv[g, 0, 2, :, ls]
                wext[rows + 3, rs, ls] = hrecv[g, 1, 2, :, ls]

        def field_row(x):
            acc = None
            for k in range(nonzero):
                term = jnp.dot(
                    wext[idx_ref[k, 0, x], rs, :],
                    mats[x, k],
                    preferred_element_type=jnp.float32,
                )
                acc = term if acc is None else acc + term
            row = acc.astype(jnp.bfloat16)
            vout[g, x, :, :] = row
            return row

        def near_only():
            settle()
            for x in range(rows // 2):
                field_row(x)

            @pl.when(has_below)
            def _():
                hand_down(g, 0).start()

            for x in range(rows // 2, rows):
                field_row(x)

        def with_far(edge, inward):
            settle()
            v = [field_row(edge + i * inward) for i in range(3)]
            scale = gq_next[rs, :]
            first = 0 if inward > 0 else 1
            fsend[g, 0, :, :] = v[0]
            for c in range(2):
                ls = slice(c * block, (c + 1) * block)
                v0, v1, v2 = (row[:, ls].astype(jnp.float32) for row in v)
                source = s_next[first, rs, ls].astype(jnp.float32)
                fsend[g, 1, :, ls] = (source - scale * (v1 + beside(v0))).astype(jnp.bfloat16)
                source = s_next[1 - first, rs, ls].astype(jnp.float32)
                fsend[g, 2, :, ls] = (source - scale * (v0 + v2 + beside(v1))).astype(jnp.bfloat16)
            for i in range(3, rows):
                field_row(edge + i * inward)
            to_partner(g).start()

        @pl.when(far_left & has_below)
        def _():
            with_far(0, 1)

        @pl.when(far_right & has_below)
        def _():
            with_far(rows - 1, -1)

        @pl.when(jnp.logical_not(is_far & has_below))
        def _():
            near_only()

        @pl.when(is_far & has_below)
        def _():
            hand_down(g, 0).start()

        @pl.when(has_below)
        def _():
            hand_down(g, 1).start()

    def first_edges(g, carry):
        edges_out(g)
        return carry

    depth = jnp.where(is_pair, 2, jnp.where(is_far, 0, 2))
    ahead = jnp.where(top, chunks, depth)
    lax.fori_loop(0, jnp.where(top, chunks, 0), first_edges, 0)

    @pl.when(via[1])
    def _():
        def forward(g, carry):
            first_leg(g).wait_recv()
            second_leg(g).start()
            return carry

        lax.fori_loop(0, chunks, forward, 0)

    loads[3].wait()
    loads[2].wait()
    lax.fori_loop(0, rows, build, 0)

    @pl.when(is_far & has_below)
    def _():
        gq_next[...] = gain_rows(z - 1)
        hand_up.wait_recv()

    lax.fori_loop(0, jnp.where(top, 0, depth), first_edges, 0)

    def step(g, carry):
        @pl.when(g + ahead < chunks)
        def _():
            edges_out(g + ahead)

        rows_out(g)
        return carry

    halves = rhs // block
    per_half = chunks // halves
    for h in range(halves - 1):
        lax.fori_loop(h * per_half, (h + 1) * per_half, step, 0)

        @pl.when(jnp.logical_not(has_below))
        def _():
            loads[4].wait()
            finish(h)

    lax.fori_loop((halves - 1) * per_half, chunks, step, 0)

    @pl.when(has_below)
    def _():
        loads[4].wait()
        for h in range(halves - 1):
            finish(h)

    finish(halves - 1)


    @pl.when(is_far & has_above)
    def _():
        hand_up.wait_send()

    def drain(g, carry):
        @pl.when(has_below)
        def _():
            hand_down(g, 0).wait_send()
            hand_down(g, 1).wait_send()

        @pl.when(is_far & has_below)
        def _():
            to_partner(g).wait_send()

        @pl.when(send_left)
        def _():
            to_left(g).wait_send()

        @pl.when(send_right)
        def _():
            to_right(g).wait_send()

        @pl.when(via[0])
        def _():
            first_leg(g).wait_send()

        @pl.when(via[1])
        def _():
            second_leg(g).wait_send()

        return carry

    lax.fori_loop(0, chunks, drain, 0)


def copy_kernel(adjoint_in, gradient_in, adjoint_out, gradient_out, sem):
    rows = adjoint_in.shape[2]
    copies = [pltpu.make_async_copy(gradient_in, gradient_out, sem.at[2 * rows])]
    for c in range(2):
        for x in range(rows):
            copies.append(
                pltpu.make_async_copy(
                    adjoint_in.at[c, 0, x], adjoint_out.at[c, 0, x], sem.at[c * rows + x]
                )
            )
    for copy in copies:
        copy.start()
    for copy in copies:
        copy.wait()


def on_device(sweeps, tiles, adjoint_source, forward_field, factor_blocks, factor_index, pml_thickness):
    _, layers, rows, block, rhs = adjoint_source.shape
    assert layers == 1
    nonzero = factor_blocks.shape[2]
    wide = 2 * block
    chunks = rhs // CHUNK
    bf16 = jnp.bfloat16
    f32 = jnp.float32
    hbm_spec = pl.BlockSpec(memory_space=pltpu.HBM)
    vmem_spec = pl.BlockSpec(memory_space=pltpu.VMEM)
    index = jnp.transpose(factor_index, (2, 0, 1))
    thickness = pml_thickness[None]
    outs = (
        jax.ShapeDtypeStruct(adjoint_source.shape, bf16),
        jax.ShapeDtypeStruct((1, rows, block), f32),
    )
    fields = pl.pallas_call(
        functools.partial(sweep_kernel, sweeps, tiles),
        out_shape=outs,
        in_specs=[hbm_spec] * 5,
        out_specs=(vmem_spec, vmem_spec),
        scratch_shapes=[
            pltpu.SMEM(index.shape, jnp.int32),
            pltpu.VMEM(thickness.shape, jnp.int32),
            pltpu.VMEM(adjoint_source.shape, bf16),
            pltpu.VMEM(forward_field.shape, bf16),
            pltpu.VMEM(factor_blocks.shape, bf16),
            pltpu.VMEM((rows, rhs, wide), bf16),
            pltpu.VMEM((2, rhs, wide), bf16),
            pltpu.VMEM((rhs, block), f32),
            pltpu.VMEM((rhs, block), f32),
            pltpu.VMEM((rows, nonzero, wide, wide), bf16),
            pltpu.VMEM((chunks, rows, CHUNK, wide), bf16),
            pltpu.VMEM((chunks, rows, CHUNK, wide), bf16),
            pltpu.VMEM((2, rhs, wide), f32),
            pltpu.VMEM((rows + 4, rhs, wide), bf16),
            pltpu.VMEM((chunks, 2, 3, CHUNK, wide), bf16),
            pltpu.VMEM((chunks, 3, CHUNK, wide), bf16),
            pltpu.VMEM((chunks, 2, 3, CHUNK, wide), bf16),
            pltpu.SemaphoreType.DMA((5,)),
            pltpu.SemaphoreType.DMA((2,)),
            pltpu.SemaphoreType.DMA((2, chunks)),
            pltpu.SemaphoreType.DMA((2, chunks)),
            pltpu.SemaphoreType.DMA((2, chunks)),
            pltpu.SemaphoreType.DMA((2, chunks)),
            pltpu.SemaphoreType.DMA((chunks,)),
            pltpu.SemaphoreType.DMA((chunks,)),
            pltpu.VMEM((chunks, 2, CHUNK, wide), bf16),
            pltpu.SemaphoreType.DMA((4, chunks)),
        ],
        compiler_params=pltpu.CompilerParams(
            collective_id=0, has_side_effects=True, vmem_limit_bytes=32 * 1024 * 1024
        ),
    )(*(
        pltpu.with_memory_space_constraint(operand, pltpu.HBM)
        for operand in (index, thickness, adjoint_source, factor_blocks, forward_field)
    ))
    return pl.pallas_call(
        copy_kernel,
        out_shape=outs,
        in_specs=[vmem_spec] * 2,
        out_specs=(hbm_spec, hbm_spec),
        scratch_shapes=[pltpu.SemaphoreType.DMA((2 * rows + 1,))],
        compiler_params=pltpu.CompilerParams(vmem_limit_bytes=4 * 1024 * 1024),
    )(*fields)


def solution(mesh):
    placed = (
        P(None, "sweep", "tile", None, None),
        P(None, "sweep", "tile", None, None),
        P("sweep", "tile", None, None, None, None),
        P("sweep", "tile", None),
        P(),
    )
    return jax.shard_map(
        functools.partial(on_device, mesh.shape["sweep"], mesh.shape["tile"]),
        mesh=mesh,
        in_specs=placed,
        out_specs=(P(None, "sweep", "tile", None, None), P("sweep", "tile", None)),
        check_vma=False,
    )
```
